32 devices in a mesh: expert: 16 (over z, x, core), dp: 2 (over y).
Axes of the slice: x: 2, y: 2, z: 4, core: 2. Of those that a mesh axis runs over, the one named last changes fastest.
Arguments:
- tokens: bfloat16 [3072, 2048], P(('expert', 'dp')), may hold values from -6 to 6
- norm_gain: float32 [2048], replicated, may hold values from 0.1 to 1.9
- expert_ids: int32 [3072, 8], P(('expert', 'dp')), may hold values from 0 to 31, all different within a row; in each aligned block of 96 rows (0 to 95, 96 to 191, ...) at most 32 rows name the same one
- route_weights: float32 [3072, 8], P(('expert', 'dp')), may hold values from 0.05 to 1
- gate_weight: bfloat16 [32, 2048, 768], P('expert', 'dp'), may hold values from -0.125 to 0.125
- up_weight: bfloat16 [32, 2048, 768], P('expert', 'dp'), may hold values from -0.125 to 0.125
- down_weight: bfloat16 [32, 768, 2048], P('expert', 'dp'), may hold values from -0.21875 to 0.21875
- pair_list: int32 [16], replicated, may hold values from 0 to 15, as said below
Outputs:
- mixed: bfloat16 [3072, 2048], P(('expert', 'dp'))
- held_gate: bfloat16 [16, 2048, 768], P('expert', 'dp')
- held_up: bfloat16 [16, 2048, 768], P('expert', 'dp')
- held_down: bfloat16 [16, 768, 2048], P('expert', 'dp')
The draws below stay inside these ranges and needn't reach their ends.
Inputs may be any that keep to these rules, and one draw needn't show every extreme that they name: pair_list[pair_list[e]] = e, and pair_list[e] is e itself or differs from e in exactly one bit. `expert_ids`: each row names 8 different experts; among the rows of one device no expert is named more than 32 times, and in every draw some device's rows name one expert exactly 32 times.
All inputs are finite; a program needn't handle non-finite values.
Results may differ from the reference program's by a relative error of at most 0.0075.
Values may be sent and summed in bfloat16 or wider, within the bound.
A program may use at most 192 MiB of HBM per device.

```python
import math
import jax
import jax.numpy as jnp
import numpy as np
from jax import lax

D = 2048
FF = 768
TOP = 8
EXP_DEV = 2
TOK_DEV = 96
EXPERTS = 32
MOST = 32
TOKENS = 3072
BITS = 4
N_EXPERT = 16
N_DP = 2


def draw_pair_list(key, part):
    positions = jnp.arange(N_EXPERT, dtype=jnp.int32)
    partners = positions
    for bit_number in range(BITS):
        tosses = jax.random.randint(jax.random.fold_in(key, 17 + bit_number), (N_EXPERT,), 0, 4)
        counterpart = jnp.bitwise_xor(positions, 1 << bit_number)
        lowest = jnp.minimum(positions, counterpart)
        unmatched = partners == positions
        chosen = (tosses[lowest] == 0) & unmatched & unmatched[counterpart]
        partners = jnp.where(chosen, counterpart, partners)
    return partners.astype(jnp.int32)


def block_levels(own_key, shape, split, smallest, top_value):
    def one(axis_at, shards_of):
        steps = jax.random.uniform(jax.random.fold_in(jax.random.fold_in(own_key, 6), axis_at), (shards_of,), jnp.float32, smallest / len(split), top_value / len(split))
        return jnp.repeat(jnp.exp(steps), shape[axis_at] // shards_of).reshape((-1,) + (1,) * (len(shape) - axis_at - 1))

    level = one(*split[0])
    for cut in split[1:]:
        level = level * one(*cut)
    return level


def shared_out(own_key, own, number, rows, number_of, top, bound, skew):
    ranking = jax.random.permutation(own_key, number_of)
    packed, ordinary = portions_of(number_of, rows * top, bound, skew, True), portions_of(number_of, rows * top, bound, skew, False)
    places = jnp.arange(number_of)

    def named(sizes, rotation):
        used = int((sizes > 0).sum())
        fixed = max(1, used // 4)
        passed = fixed + (places - fixed + rotation * (used - fixed)) % max(1, number_of - fixed)
        return jnp.zeros((number_of,), jnp.int32).at[ranking[jnp.where(places < fixed, places, passed)]].set(jnp.asarray(sizes, jnp.int32))

    sizes = jnp.where(number % 4 == 0, named(packed, number // 4), named(ordinary, number - number // 4 - 1))
    mixed = jax.random.permutation(jax.random.fold_in(own, 3), number_of)
    donor, sink = mixed[0:number_of // 2 * 2:2], mixed[1:number_of // 2 * 2:2]
    room = jnp.minimum(sizes[donor] - 1, bound - sizes[sink]) // 2
    room = jnp.where((donor == ranking[0]) | (sink == ranking[0]) | (sizes[sink] == 0), 0, jnp.maximum(room, 0))
    passed = jax.random.randint(jax.random.fold_in(own, 4), (number_of // 2,), 0, 1 << 20) % (room + 1)
    sizes = sizes.at[donor].add(-passed).at[sink].add(passed)
    items = jnp.searchsorted(jnp.cumsum(sizes), jnp.arange(rows * top), side="right").astype(jnp.int32)
    listing = items.reshape(top, rows).T
    listing = listing[jax.random.permutation(jax.random.fold_in(own, 1), rows)]
    rotation = jax.random.randint(jax.random.fold_in(own, 2), (rows, 1), 0, top)
    return jnp.take_along_axis(listing, (jnp.arange(top)[None, :] + rotation) % top, axis=1)


def portions_of(number_of, total, reach, slope, full):
    loads = [(1 << 20) // math.isqrt(rank ** slope) + 1 for rank in range(1, number_of + 1)]
    largest = reach if full else min(reach, max(-(-total // number_of), total * loads[0] // sum(loads)))
    least = 1 if total - largest >= number_of - 1 else 0
    counts, spare = [largest] + [least] * (number_of - 1), total - largest - least * (number_of - 1)
    while spare > 0:
        candidates = [i for i in range(1, number_of) if counts[i] < largest] or [i for i in range(1, number_of) if counts[i] < reach]
        pool, budget = sum([loads[i] for i in candidates]), spare
        for i in candidates:
            extra = min(reach - counts[i], max(1, budget * loads[i] // pool), spare)
            counts[i] = counts[i] + extra
            spare = spare - extra
    return np.array(counts)


def normal_values(rng, shape, spread, most, split=(), kind=jnp.bfloat16):
    drawn = jax.random.normal(rng, shape, jnp.float32) * spread
    if len(split) > 0:
        drawn = block_levels(rng, shape, split, -0.22, 0.18) * drawn
    return jnp.clip(drawn, min=-most, max=most).astype(kind)


def setup_inputs(seed: int = 0) -> dict:
    splits = jax.random.split(jax.random.key(seed), 9)
    tokens = normal_values(splits[0], (TOKENS, D), 1.0, 6.0, ((0, 32),))
    norm_gain = jnp.clip(1.0 + 0.18 * jax.random.normal(splits[1], (D,), jnp.float32), 0.1, 1.9)
    expert_ids_keys = jax.random.split(jax.random.fold_in(splits[2], 1), TOKENS // TOK_DEV)
    expert_ids_turns = jax.random.permutation(jax.random.fold_in(splits[2], 3), TOKENS // TOK_DEV)
    expert_ids = jax.vmap(lambda own, number: shared_out(jax.random.fold_in(splits[2], 2), own, number, TOK_DEV, EXPERTS, TOP, MOST, 2))(expert_ids_keys, expert_ids_turns).reshape((TOKENS, TOP))
    route_weights = jnp.clip(0.05 + 0.95 * jax.random.uniform(splits[3], (TOKENS, TOP), jnp.float32) ** block_levels(splits[3], (TOKENS, TOP), ((0, 32),), -0.2, 0.2), 0.05, 1.0)
    gate_weight = normal_values(splits[4], (EXPERTS, D, FF), D ** -0.5, 0.125, ((0, 16), (1, 2)))
    up_weight = normal_values(splits[5], (EXPERTS, D, FF), D ** -0.5, 0.125, ((0, 16), (1, 2)))
    down_weight = normal_values(splits[6], (EXPERTS, FF, D), FF ** -0.5, 0.21875, ((0, 16), (1, 2)))
    pair_list = draw_pair_list(jax.random.fold_in(splits[8], 71), 0)
    return dict(tokens=tokens, norm_gain=norm_gain, expert_ids=expert_ids, route_weights=route_weights, gate_weight=gate_weight, up_weight=up_weight, down_weight=down_weight, pair_list=pair_list)


def reference(tokens, norm_gain, expert_ids, route_weights, gate_weight, up_weight, down_weight, pair_list):
    values = tokens.astype(jnp.float32)
    scale = lax.rsqrt(lax.optimization_barrier(jnp.mean(values * values, axis=-1, keepdims=True)) + 1e-06)
    normed = (values * scale * norm_gain).astype(jnp.bfloat16)
    flat_ids = expert_ids.reshape(-1)
    flat_weights = lax.optimization_barrier(route_weights.reshape(-1).astype(jnp.bfloat16)).astype(jnp.float32)
    capacity = N_EXPERT * N_DP * MOST

    def one_expert(expert, total):
        matching = flat_ids == expert
        chosen = jnp.nonzero(matching, size=capacity, fill_value=0)[0].astype(jnp.int32)
        number = jnp.sum(matching.astype(jnp.int32))
        valid = jnp.arange(capacity, dtype=jnp.int32) < number
        token_rows = (chosen // TOP).astype(jnp.int32)
        inputs = normed[token_rows]
        gate_act = jnp.dot(inputs, gate_weight[expert], preferred_element_type=jnp.float32)
        up_act = jnp.dot(inputs, up_weight[expert], preferred_element_type=jnp.float32)
        hidden = (jax.nn.silu(gate_act) * up_act).astype(jnp.bfloat16)
        result = jnp.dot(hidden, down_weight[expert], preferred_element_type=jnp.float32)
        result = lax.optimization_barrier(result.astype(jnp.bfloat16)).astype(jnp.float32)
        factor = jnp.where(valid, flat_weights[chosen], jnp.zeros((), jnp.float32))
        return total.at[token_rows].add(result * factor[:, None])
    total = lax.fori_loop(0, EXPERTS, one_expert, jnp.zeros((TOKENS, D), jnp.float32))
    mixed = total.astype(jnp.bfloat16)
    source = (EXP_DEV * pair_list).astype(jnp.int32)
    return (mixed, gate_weight[source], up_weight[source], down_weight[source])
```

```python
import jax
import jax.numpy as jnp
from jax import lax
from jax.sharding import PartitionSpec as P

F32 = jnp.float32
BF16 = jnp.bfloat16


def bit_route(count, bit):
    return [(e, e ^ (1 << bit)) for e in range(count) if e ^ (1 << bit) < count]


def swap_branch(bits, count):
    def run(blocks, distance):
        out = blocks
        for bit in bits:
            arrived = [lax.ppermute(b, "expert", bit_route(count, bit)) for b in blocks]
            out = [jnp.where(distance == (1 << bit), a, o) for a, o in zip(arrived, out)]
        return tuple(out)

    return run


def swap(blocks, pair_list, count, bit_total):
    mine = lax.axis_index("expert")
    places = jnp.arange(count, dtype=jnp.int32)
    distances = jnp.bitwise_xor(pair_list, places)
    distance = jnp.bitwise_xor(pair_list[mine], mine)
    choice = jnp.int32(0)
    for bit in range(1, bit_total):
        used = jnp.any(distances == (1 << bit)).astype(jnp.int32)
        choice = choice + (used << (bit - 1))
    branches = []
    for mask in range(1 << (bit_total - 1)):
        bits = [0] + [b for b in range(1, bit_total) if mask >> (b - 1) & 1]
        branches.append(swap_branch(bits, count))
    return lax.switch(choice, branches, list(blocks), distance)


def placing_of(ids, parity, count, per_device, capacity):
    rows = ids.shape[0]
    experts = jnp.arange(count, dtype=jnp.int32) * per_device + parity
    equal = ids[:, :, None] == experts[None, None, :]
    member = jnp.any(equal, axis=1)
    lower = jnp.tril(jnp.ones((rows, rows), BF16), -1)
    rank = jnp.dot(lower, member.astype(BF16), preferred_element_type=F32).astype(jnp.int32)
    rank = jnp.where(member, rank, -1)
    slots = jnp.arange(capacity, dtype=jnp.int32)
    hit = rank.T[:, None, :] == slots[None, :, None]
    return equal, hit


def body(
    tokens, norm_gain, expert_ids, route_weights, gate_weight, up_weight, down_weight, pair_list
):
    count = lax.axis_size("expert")
    dp = lax.axis_size("dp")
    per_device = gate_weight.shape[0]
    group = per_device if dp % per_device == 0 else 1
    experts_all = count * per_device
    rows, top = expert_ids.shape
    width = tokens.shape[1]
    capacity = max(2, 4 * rows * top // (3 * experts_all))
    d = lax.axis_index("dp")
    parity = d % group

    values = tokens.astype(F32)
    scale = lax.rsqrt(jnp.mean(values * values, axis=-1, keepdims=True) + 1e-06)
    normed = (values * scale * norm_gain).astype(BF16)
    route_bf = route_weights.astype(BF16)

    def in_group(block, shift):
        if shift % group == 0:
            return block
        route = [(i, i // group * group + (i % group + shift) % group) for i in range(dp)]
        return lax.ppermute(block, "dp", route)

    token_sets = [
        (in_group(normed, s), in_group(expert_ids, s), in_group(route_bf, s)) for s in range(group)
    ]
    token_sets, weights = lax.optimization_barrier(
        (token_sets, (gate_weight, up_weight, down_weight))
    )

    def shards(weight):
        out = []
        for s in range(dp):
            sent = lax.dynamic_index_in_dim(weight, (d + s) % group, 0, keepdims=False)
            if s:
                sent = lax.ppermute(sent, "dp", [(i, (i + s) % dp) for i in range(dp)])
            out.append(sent)
        return out

    gates, ups, downs = [shards(w) for w in weights]

    outgoing, weightings = [], []
    for normed_s, ids_s, route_s in token_sets:
        equal, hit = placing_of(ids_s, parity, count, per_device, capacity)
        picked = jnp.dot(
            hit.reshape(count * capacity, rows).astype(BF16), normed_s, preferred_element_type=F32
        ).astype(BF16)
        outgoing.append(picked.reshape(count, capacity, width))
        factor = jnp.sum(jnp.where(equal, route_s[:, :, None], jnp.zeros((), BF16)), axis=1)
        weightings.append(
            jnp.where(hit, factor.T[:, None, :], jnp.zeros((), BF16)).reshape(
                count * capacity, rows
            )
        )
    outgoing = jnp.concatenate(outgoing, axis=1)
    received = lax.all_to_all(outgoing, "expert", split_axis=0, concat_axis=0, tiled=True)
    columns = received.reshape(count * group * capacity, width)

    held = swap([gate_weight[0], up_weight[0], down_weight[0]], pair_list, count,
                count.bit_length() - 1)

    def times(x, parts):
        size = parts[0].shape[0]
        total = None
        for s, part in enumerate(parts):
            at = (d - s) % dp
            piece = lax.dynamic_slice_in_dim(x, at * size, size, axis=1)
            term = jnp.dot(piece, part, preferred_element_type=F32)
            total = term if total is None else total + term
        return total

    hidden = (jax.nn.silu(times(columns, gates)) * times(columns, ups)).astype(BF16)
    expert_out = times(hidden, downs).astype(BF16)
    returned = lax.all_to_all(
        expert_out.reshape(count, group * capacity, width),
        "expert",
        split_axis=0,
        concat_axis=0,
        tiled=True,
    )
    total = None
    for s in range(group):
        part = returned[:, s * capacity : (s + 1) * capacity].reshape(count * capacity, width)
        mix = jnp.einsum("sr,sd->rd", weightings[s], part, preferred_element_type=F32)
        if s:
            mix = in_group(mix.astype(BF16), group - s).astype(F32)
        total = mix if total is None else total + mix
    return (total.astype(BF16), held[0][None], held[1][None], held[2][None])


def solution(mesh):
    in_specs = (
        P(("expert", "dp"), None),
        P(),
        P(("expert", "dp"), None),
        P(("expert", "dp"), None),
        P("expert", "dp", None),
        P("expert", "dp", None),
        P("expert", "dp", None),
        P(),
    )
    out_specs = (
        P(("expert", "dp"), None),
        P("expert", "dp", None),
        P("expert", "dp", None),
        P("expert", "dp", None),
    )
    return jax.shard_map(body, mesh=mesh, in_specs=in_specs, out_specs=out_specs, check_vma=False)
```

```python
import jax
import jax.numpy as jnp
from jax import lax
from jax.sharding import PartitionSpec as P

F32 = jnp.float32
BF16 = jnp.bfloat16


def bit_route(count, bit, cores):
    return [
        (e, e ^ (1 << bit)) for e in range(count) if e ^ (1 << bit) < count and (e & 1) in cores
    ]


def swap_branch(moves, count):
    def run(blocks, base, distance):
        arrived = [
            [lax.ppermute(b, "expert", bit_route(count, bit, cores)) for b in blocks]
            for bit, cores in moves
        ]
        out = base
        for (bit, _), got in zip(moves, arrived):
            out = [jnp.where(distance == (1 << bit), a, o) for a, o in zip(got, out)]
        return tuple(out)

    return run


def swap(blocks, base, pair_list, count, always, bits):
    mine = lax.axis_index("expert")
    places = jnp.arange(count, dtype=jnp.int32)
    distances = jnp.bitwise_xor(pair_list, places)
    distance = jnp.bitwise_xor(pair_list[mine], mine)
    choice = jnp.int32(0)
    for n, bit in enumerate(bits):
        for core in range(2):
            used = jnp.any((distances == (1 << bit)) & (places & 1 == core)).astype(jnp.int32)
            choice = choice + (used << (2 * n + core))
    branches = []
    for mask in range(1 << (2 * len(bits))):
        moves = [(bit, (0, 1)) for bit in always]
        for n, bit in enumerate(bits):
            cores = tuple(c for c in range(2) if mask >> (2 * n + c) & 1)
            if cores:
                moves.append((bit, cores))
        branches.append(swap_branch(moves, count))
    return list(lax.switch(choice, branches, list(blocks), list(base), distance))


def placing_of(ids, parity, count, per_device, capacity):
    rows = ids.shape[0]
    experts = jnp.arange(count, dtype=jnp.int32) * per_device + parity
    equal = ids[:, :, None] == experts[None, None, :]
    member = jnp.any(equal, axis=1)
    lower = jnp.tril(jnp.ones((rows, rows), BF16), -1)
    rank = jnp.dot(lower, member.astype(BF16), preferred_element_type=F32).astype(jnp.int32)
    rank = jnp.where(member, rank, -1)
    slots = jnp.arange(capacity, dtype=jnp.int32)
    hit = rank.T[:, None, :] == slots[None, :, None]
    return equal, hit


def body(
    tokens, norm_gain, expert_ids, route_weights, gate_weight, up_weight, down_weight, pair_list
):
    count = lax.axis_size("expert")
    dp = lax.axis_size("dp")
    per_device = gate_weight.shape[0]
    group = per_device if dp % per_device == 0 else 1
    experts_all = count * per_device
    rows, top = expert_ids.shape
    width = tokens.shape[1]
    capacity = max(2, 4 * rows * top // (3 * experts_all))
    d = lax.axis_index("dp")
    parity = d % group

    values = tokens.astype(F32)
    scale = lax.rsqrt(jnp.mean(values * values, axis=-1, keepdims=True) + 1e-06)
    normed = (values * scale * norm_gain).astype(BF16)
    route_bf = route_weights.astype(BF16)

    def in_group(block, shift):
        if shift % group == 0:
            return block
        route = [(i, i // group * group + (i % group + shift) % group) for i in range(dp)]
        return lax.ppermute(block, "dp", route)

    token_sets = [
        (in_group(normed, s), in_group(expert_ids, s), in_group(route_bf, s)) for s in range(group)
    ]
    token_sets, weights = lax.optimization_barrier(
        (token_sets, (gate_weight, up_weight, down_weight))
    )

    def shards(weight):
        out = []
        for s in range(dp):
            sent = lax.dynamic_index_in_dim(weight, (d + s) % group, 0, keepdims=False)
            if s:
                sent = lax.ppermute(sent, "dp", [(i, (i + s) % dp) for i in range(dp)])
            out.append(sent)
        return out

    gates, ups, downs = [shards(w) for w in weights]

    outgoing, weightings = [], []
    for normed_s, ids_s, route_s in token_sets:
        equal, hit = placing_of(ids_s, parity, count, per_device, capacity)
        picked = jnp.dot(
            hit.reshape(count * capacity, rows).astype(BF16), normed_s, preferred_element_type=F32
        ).astype(BF16)
        outgoing.append(picked.reshape(count, capacity, width))
        factor = jnp.sum(jnp.where(equal, route_s[:, :, None], jnp.zeros((), BF16)), axis=1)
        weightings.append(
            jnp.where(hit, factor.T[:, None, :], jnp.zeros((), BF16)).reshape(
                count * capacity, rows
            )
        )
    outgoing = jnp.concatenate(outgoing, axis=1)
    bit_total = count.bit_length() - 1
    firsts = [gate_weight[0], up_weight[0], down_weight[0]]
    early = list(range(1, min(3, bit_total)))
    late = list(range(3, bit_total))
    outgoing, pairs = lax.optimization_barrier((outgoing, pair_list))
    received = lax.all_to_all(outgoing, "expert", split_axis=0, concat_axis=0, tiled=True)
    half_held = swap(firsts, firsts, pairs, count, [], early)
    received, half_held = lax.optimization_barrier((received, half_held))
    columns = received.reshape(count * group * capacity, width)

    def times(x, parts):
        size = parts[0].shape[0]
        total = None
        for s, part in enumerate(parts):
            at = (d - s) % dp
            piece = lax.dynamic_slice_in_dim(x, at * size, size, axis=1)
            term = jnp.dot(piece, part, preferred_element_type=F32)
            total = term if total is None else total + term
        return total

    hidden = (jax.nn.silu(times(columns, gates)) * times(columns, ups)).astype(BF16)
    expert_out = times(hidden, downs).astype(BF16)
    expert_out, pairs = lax.optimization_barrier((expert_out, pairs))
    held = swap(firsts, half_held, pairs, count, [0], late)
    returned = lax.all_to_all(
        expert_out.reshape(count, group * capacity, width),
        "expert",
        split_axis=0,
        concat_axis=0,
        tiled=True,
    )
    returned, held = lax.optimization_barrier((returned, held))
    total = None
    for s in range(group):
        part = returned[:, s * capacity : (s + 1) * capacity].reshape(count * capacity, width)
        mix = jnp.einsum("sr,sd->rd", weightings[s], part, preferred_element_type=F32)
        if s:
            mix = in_group(mix.astype(BF16), group - s).astype(F32)
        total = mix if total is None else total + mix
    return (total.astype(BF16), held[0][None], held[1][None], held[2][None])


def solution(mesh):
    in_specs = (
        P(("expert", "dp"), None),
        P(),
        P(("expert", "dp"), None),
        P(("expert", "dp"), None),
        P("expert", "dp", None),
        P("expert", "dp", None),
        P("expert", "dp", None),
        P(),
    )
    out_specs = (
        P(("expert", "dp"), None),
        P("expert", "dp", None),
        P("expert", "dp", None),
        P("expert", "dp", None),
    )
    return jax.shard_map(body, mesh=mesh, in_specs=in_specs, out_specs=out_specs, check_vma=False)
```
